512 devices in a mesh: node: 64 (over y, z), local: 8 (over x, core).
Axes of the slice: x: 4, y: 4, z: 16, core: 2. Of those that a mesh axis runs over, the one named last changes fastest.
Arguments:
- grad_out: bfloat16 [65536, 3584], P(('node', 'local')), may hold values from -6 to 6
- expert_ids: int32 [65536, 8], P(('node', 'local')), may hold values from 0 to 255, as said below
- gate_weights: float32 [65536, 8], P(('node', 'local')), may hold values from 0.05 to 0.35
- saved_hidden: bfloat16 [64, 1024, 1024], P('node', None, 'local'), may hold values from -0.59765625 to 0.59765625
- down_weight: bfloat16 [64, 1024, 3584], P('node', 'local'), may hold values from -0.1875 to 0.1875
- second_moment: bfloat16 [64, 1024, 3584], P('node', 'local'), may hold values from 0.0019989014 to 0.25
Outputs:
- gate_weight_gradient: float32 [65536, 8], P(('node', 'local'))
- hidden_grad: bfloat16 [64, 1024, 1024], P('node', None, 'local')
- new_weight: bfloat16 [64, 1024, 3584], P('node', 'local')
- new_second: bfloat16 [64, 1024, 3584], P('node', 'local')
The draws below stay inside these ranges and needn't reach their ends.
Inputs may be any that keep to these rules, and one draw needn't show every extreme that they name: `expert_ids`: each row names 8 different experts on at most 4 nodes (node = id // 4), two on each; at most one per row is in flight (id % 4 == 0). Among the rows of one device at most 2 name the in-flight expert of any one node, and in every draw some node receives exactly 2 from every device.
All inputs are finite; a program needn't handle non-finite values.
Results may differ from the reference program's by a relative error of at most 0.0051.
Values may be sent and summed in bfloat16 or wider, within the bound.
No kernel may reach another device: no remote copies, remote signals or barrier semaphores. Data moves between devices by JAX's collectives and lax.ppermute only.
A program may use at most 128 MiB of HBM per device.

```python
import math
import jax
import jax.numpy as jnp
from jax import lax

D = 3584
H_WIN = 1024
EXPERTS_PER_HOST = 4
CHOSEN_EXPERTS = 8
MAX_NODES = 4
TOK_DEV = 128
CAP = 2
SLOTS = 1024
TOTAL_TOKENS = 65536
N_NODE = 64
N_LOCAL = 8


def draw_expert_ids(key, part):
    device_count = N_NODE * N_LOCAL
    token_count = device_count * TOK_DEV
    keys = jax.random.split(key, 8)
    hot_rank = jax.random.permutation(keys[0], N_NODE)
    hot_nodes = hot_rank < max(N_NODE // 8, 1)
    counts = jax.random.randint(keys[1], (device_count, N_NODE), 0, CAP)
    counts = jnp.where(hot_nodes[None, :], CAP, counts)
    order_key = jax.random.randint(keys[2], (device_count, N_NODE), 0, 1 << 20) * N_NODE + jnp.arange(N_NODE)[None, :]
    order = jnp.argsort(order_key, axis=1)
    ordered = jnp.take_along_axis(counts, order, 1)
    ends = jnp.cumsum(ordered, 1)
    position = jnp.arange(TOK_DEV)
    slot_node = jnp.sum((position[None, :, None] >= ends[:, None, :]).astype(jnp.int32), 2)
    valid = slot_node < N_NODE
    listed = jnp.take_along_axis(order, jnp.minimum(slot_node, N_NODE - 1), 1)
    listed = jnp.where(valid, listed, -1)
    shuffle_key = jax.random.randint(keys[3], (device_count, TOK_DEV), 0, 1 << 20) * TOK_DEV + jnp.arange(TOK_DEV)[None, :]
    shuffle = jnp.argsort(shuffle_key, axis=1)
    hit_node = jnp.take_along_axis(listed, shuffle, 1).reshape(token_count)
    node_score = jax.random.randint(keys[4], (token_count, N_NODE), 0, 1 << 16) * N_NODE + jnp.arange(N_NODE)[None, :]
    node_score = node_score + jnp.where(jnp.arange(N_NODE)[None, :] == hit_node[:, None], 1 << 24, 0)
    scores_top, picked_experts = lax.top_k(node_score, MAX_NODES)
    first_pick = jax.random.randint(keys[5], (token_count, MAX_NODES), 0, EXPERTS_PER_HOST - 1)
    second_pick = jax.random.randint(keys[6], (token_count, MAX_NODES), 0, EXPERTS_PER_HOST - 2)
    slot_first = 1 + first_pick
    slot_second = 1 + (first_pick + 1 + second_pick) % (EXPERTS_PER_HOST - 1)
    is_hit = (jnp.arange(MAX_NODES)[None, :] == 0) & (hit_node[:, None] >= 0)
    slot_first = jnp.where(is_hit, 0, slot_first)
    chosen_ids = jnp.concatenate([picked_experts * EXPERTS_PER_HOST + slot_first, picked_experts * EXPERTS_PER_HOST + slot_second], 1)
    column_key = jax.random.randint(keys[7], (token_count, CHOSEN_EXPERTS), 0, 1 << 16) * CHOSEN_EXPERTS + jnp.arange(CHOSEN_EXPERTS)[None, :]
    chosen_ids = jnp.take_along_axis(chosen_ids, jnp.argsort(column_key, axis=1), 1)
    return chosen_ids.astype(jnp.int32)


def block_scale(stream_key, shape, cuts, least, top_value):
    def one(dim, parts):
        heights = jax.random.uniform(jax.random.fold_in(jax.random.fold_in(stream_key, 6), dim), (parts,), jnp.float32, least / len(cuts), top_value / len(cuts))
        return jnp.repeat(jnp.exp(heights), shape[dim] // parts).reshape((-1,) + (1,) * (len(shape) - dim - 1))

    level = one(*cuts[0])
    for cut in cuts[1:]:
        level = level * one(*cut)
    return level


def centred(own_key, dims, spread, reach, shards=(), kind=jnp.bfloat16):
    drawn = jax.random.normal(own_key, dims, jnp.float32) * spread
    if len(shards) > 0:
        drawn = block_scale(own_key, dims, shards, -0.22, 0.18) * drawn
    return jnp.clip(drawn, min=-reach, max=reach).astype(kind)


def setup_inputs(seed: int = 0) -> dict:
    splits = jax.random.split(jax.random.key(seed), 7)
    return {
        "grad_out": centred(splits[0], (TOTAL_TOKENS, D), 1.0, 6.0, ((0, 512),)),
        "expert_ids": draw_expert_ids(jax.random.fold_in(splits[6], 71), 0),
        "gate_weights": jnp.clip(0.05 + 0.29999999 * jax.random.uniform(splits[2], (TOTAL_TOKENS, CHOSEN_EXPERTS), jnp.float32) ** block_scale(splits[2], (TOTAL_TOKENS, CHOSEN_EXPERTS), ((0, 512),), -0.2, 0.2), 0.05, 0.35),
        "saved_hidden": centred(splits[3], (N_NODE, SLOTS, H_WIN), 0.1, 0.59765625, ((0, 64), (2, 8))),
        "down_weight": centred(splits[4], (N_NODE, H_WIN, D), H_WIN ** -0.5, 0.1875, ((0, 64), (1, 8))),
        "second_moment": jnp.clip(jnp.exp(math.log(0.25) - 4.828863 * jax.random.uniform(splits[5], (N_NODE, H_WIN, D), jnp.float32) ** block_scale(splits[5], (N_NODE, H_WIN, D), ((0, 64), (1, 8)), -0.2, 0.2)), 0.0019989014, 0.25).astype(jnp.bfloat16),
    }


beta_second = 0.95
learn_rate = 0.002
decay_rate = 0.1
epsilon = 1e-08
correct_second = 0.994079470779666

def pack_device(picked_experts, gate_values, grads):
    transit_rows = picked_experts % EXPERTS_PER_HOST == 0
    row_present = jnp.any(transit_rows, 1)
    destination_node = lax.optimization_barrier(jnp.sum(jnp.where(transit_rows, picked_experts // EXPERTS_PER_HOST, 0), 1)).astype(jnp.int32)
    onehot = ((destination_node[:, None] == jnp.arange(N_NODE, dtype=jnp.int32)[None, :]) & row_present[:, None]).astype(jnp.int32)
    within_rank = lax.optimization_barrier(jnp.sum(onehot * (jnp.cumsum(onehot, 0) - 1), 1)).astype(jnp.int32)
    slot_index = destination_node * CAP + within_rank
    expert_location = (jnp.arange(N_NODE * CAP, dtype=jnp.int32)[:, None] == slot_index[None, :]) & row_present[None, :]
    matched_gate = lax.optimization_barrier(jnp.sum(jnp.where(transit_rows, gate_values, 0.0), 1)).astype(jnp.bfloat16)
    departing_rows = jnp.dot(expert_location.astype(jnp.bfloat16), grads, preferred_element_type=jnp.float32).astype(jnp.bfloat16)
    departing_gates = lax.optimization_barrier(jnp.sum(jnp.where(expert_location, matched_gate.astype(jnp.float32)[None, :], 0.0), 1)).astype(jnp.bfloat16)
    return (departing_rows, departing_gates, expert_location, transit_rows)

def reference(grad_out, expert_ids, gate_weights, saved_hidden, down_weight, second_moment):
    device_count = N_NODE * N_LOCAL
    bundled_rows = lax.map(lambda item: pack_device(item[0], item[1], item[2]), (expert_ids.reshape(device_count, TOK_DEV, CHOSEN_EXPERTS), gate_weights.reshape(device_count, TOK_DEV, CHOSEN_EXPERTS), grad_out.reshape(device_count, TOK_DEV, D)))
    departing_rows, departing_gates, expert_location, transit_rows = bundled_rows
    departing_rows = departing_rows.reshape(N_NODE, N_LOCAL, N_NODE, CAP, D)
    departing_gates = departing_gates.reshape(N_NODE, N_LOCAL, N_NODE, CAP)

    def per_node(item):
        node_id, weight_now, second_now, hidden_now = item
        arrived = jnp.take(departing_rows, node_id, axis=2)
        arrived = jnp.transpose(arrived, (1, 0, 2, 3)).reshape(SLOTS, D)
        slot_gates = jnp.transpose(jnp.take(departing_gates, node_id, axis=2), (1, 0, 2)).reshape(SLOTS).astype(jnp.float32)
        unscaled = lax.dot_general(arrived, weight_now, (((1,), (1,)), ((), ())), preferred_element_type=jnp.float32)
        hidden_out = (slot_gates[:, None] * unscaled).astype(jnp.bfloat16)
        slot_score = lax.optimization_barrier(jnp.sum(unscaled * hidden_now.astype(jnp.float32), 1))
        scaled = (slot_gates[:, None] * arrived.astype(jnp.float32)).astype(jnp.bfloat16)
        grad = lax.dot_general(hidden_now, scaled, (((0,), (0,)), ((), ())), preferred_element_type=jnp.float32)
        second_new = beta_second * second_now.astype(jnp.float32) + (1.0 - beta_second) * grad * grad
        weight_f = weight_now.astype(jnp.float32)
        update = grad / (jnp.sqrt(second_new / correct_second) + epsilon) + decay_rate * weight_f
        weight_new = weight_f - learn_rate * update
        return (slot_score, hidden_out, weight_new.astype(jnp.bfloat16), second_new.astype(jnp.bfloat16))
    scores, hidden_grad, new_weight, new_second = lax.map(per_node, (jnp.arange(N_NODE, dtype=jnp.int32), down_weight, second_moment, saved_hidden))
    scores = scores.reshape(N_NODE, N_LOCAL, N_NODE, CAP)
    returned = jnp.transpose(scores, (2, 1, 0, 3)).reshape(device_count, N_NODE * CAP)
    token_gradient = lax.optimization_barrier(jnp.sum(jnp.where(expert_location, returned[:, :, None], 0.0), 1))
    gate_weight_gradient = jnp.where(transit_rows, token_gradient[:, :, None], 0.0).reshape(TOTAL_TOKENS, CHOSEN_EXPERTS)
    return (gate_weight_gradient, hidden_grad, new_weight, new_second)
```

```python
import jax
import jax.numpy as jnp
from jax import lax
from jax.sharding import PartitionSpec as P

EXPERTS_PER_HOST = 4
CAP = 2


beta_second = 0.95
learn_rate = 0.002
decay_rate = 0.1
epsilon = 1e-08
correct_second = 0.994079470779666


def route(picked_experts, gate_values, node_count):
    transit_rows = picked_experts % EXPERTS_PER_HOST == 0
    row_present = jnp.any(transit_rows, 1)
    destination_node = jnp.sum(jnp.where(transit_rows, picked_experts // EXPERTS_PER_HOST, 0), 1)
    tokens = picked_experts.shape[0]
    same = (
        (destination_node[:, None] == destination_node[None, :])
        & row_present[None, :]
        & (jnp.arange(tokens)[None, :] < jnp.arange(tokens)[:, None])
    )
    within_rank = jnp.sum(same.astype(jnp.int32), 1)
    slot_index = destination_node * CAP + within_rank
    expert_location = (
        jnp.arange(node_count * CAP, dtype=jnp.int32)[:, None] == slot_index[None, :]
    ) & row_present[None, :]
    matched_gate = jnp.sum(jnp.where(transit_rows, gate_values, 0.0), 1).astype(jnp.bfloat16)
    return expert_location, transit_rows, row_present, matched_gate.astype(jnp.float32)


def on_device(grad_out, expert_ids, gate_weights, saved_hidden, down_weight, second_moment):
    node_count = lax.axis_size("node")
    members = lax.axis_size("local")
    feature_count = grad_out.shape[1]
    expert_location, transit_rows, row_present, gate = route(expert_ids, gate_weights, node_count)
    slot_gate = jnp.sum(jnp.where(expert_location, gate[None, :], 0.0), 1)
    picked = jnp.dot(expert_location.astype(jnp.bfloat16), grad_out, preferred_element_type=jnp.float32)
    scaled_out = (slot_gate[:, None] * picked).astype(jnp.bfloat16)
    arrived = lax.all_to_all(
        scaled_out.reshape(node_count, CAP, feature_count), "node", split_axis=0, concat_axis=0, tiled=True
    )
    scaled = lax.all_gather(arrived.reshape(node_count * CAP, feature_count), "local", axis=0, tiled=True)
    weight_now = down_weight[0]
    hidden_now = saved_hidden[0]
    hidden_f = lax.dot_general(
        scaled, weight_now, (((1,), (1,)), ((), ())), preferred_element_type=jnp.float32
    )
    slot_score = jnp.sum(hidden_f * hidden_now.astype(jnp.float32), 1)
    grad = lax.dot_general(
        hidden_now, scaled, (((0,), (0,)), ((), ())), preferred_element_type=jnp.float32
    )
    second_new = (
        beta_second * second_moment[0].astype(jnp.float32) + (1.0 - beta_second) * grad * grad
    )
    weight_f = weight_now.astype(jnp.float32)
    update = grad / (jnp.sqrt(second_new / correct_second) + epsilon) + decay_rate * weight_f
    weight_new = weight_f - learn_rate * update
    score_terms = slot_score.reshape(members, node_count * CAP)
    summed = lax.psum(score_terms, "local")
    own_terms = lax.dynamic_slice_in_dim(summed, lax.axis_index("local"), 1, 0)
    returned = lax.all_to_all(
        own_terms.reshape(node_count, CAP), "node", split_axis=0, concat_axis=0, tiled=True
    )
    returned_flat = returned.reshape(node_count * CAP)
    token_score = jnp.sum(jnp.where(expert_location, returned_flat[:, None], 0.0), 0)
    token_gradient = jnp.where(row_present, token_score / jnp.where(row_present, gate, 1.0), 0.0)
    gate_weight_gradient = jnp.where(transit_rows, token_gradient[:, None], 0.0)
    return (
        gate_weight_gradient,
        hidden_f.astype(jnp.bfloat16)[None],
        weight_new.astype(jnp.bfloat16)[None],
        second_new.astype(jnp.bfloat16)[None],
    )


def solution(mesh):
    return jax.shard_map(
        on_device,
        mesh=mesh,
        in_specs=(
            P(("node", "local"), None),
            P(("node", "local"), None),
            P(("node", "local"), None),
            P("node", None, "local"),
            P("node", "local", None),
            P("node", "local", None),
        ),
        out_specs=(
            P(("node", "local"), None),
            P("node", None, "local"),
            P("node", "local", None),
            P("node", "local", None),
        ),
        check_vma=False,
    )
```

```python
import functools
import jax
import jax.numpy as jnp
from jax import lax
from jax.experimental import pallas as pl
from jax.experimental.pallas import tpu as pltpu
from jax.sharding import PartitionSpec as P

EXPERTS_PER_HOST = 4
CAP = 2
TILE = 896
VMEM_BYTES = 12 << 20


beta_second = 0.95
learn_rate = 0.002
decay_rate = 0.1
epsilon = 1e-08
correct_second = 0.994079470779666


def route(picked_experts, gate_values, node_count):
    transit_rows = picked_experts % EXPERTS_PER_HOST == 0
    row_present = jnp.any(transit_rows, 1)
    destination_node = jnp.sum(jnp.where(transit_rows, picked_experts // EXPERTS_PER_HOST, 0), 1)
    tokens = picked_experts.shape[0]
    same = (
        (destination_node[:, None] == destination_node[None, :])
        & row_present[None, :]
        & (jnp.arange(tokens)[None, :] < jnp.arange(tokens)[:, None])
    )
    within_rank = jnp.sum(same.astype(jnp.int32), 1)
    slot_index = destination_node * CAP + within_rank
    expert_location = (
        jnp.arange(node_count * CAP, dtype=jnp.int32)[:, None] == slot_index[None, :]
    ) & row_present[None, :]
    matched_gate = jnp.sum(jnp.where(transit_rows, gate_values, 0.0), 1).astype(jnp.bfloat16)
    return expert_location, transit_rows, row_present, matched_gate.astype(jnp.float32)


def gather_near(block):
    members = lax.axis_size("local")
    up = [(i, (i + 2) % members) for i in range(members)]
    down = [(i, (i - 2) % members) for i in range(members)]
    swap = [(i, i ^ 1) for i in range(members)]
    low = lax.ppermute(block, "local", up)
    high = lax.ppermute(block, "local", down)
    other = lax.ppermute(block, "local", swap)
    return block, other, low, high


def gather_more(low, high, core):
    members = lax.axis_size("local")
    onward = [(i, (i + (2 if i % 2 == 0 else -2)) % members) for i in range(members)]
    swap = [(i, i ^ 1) for i in range(members)]
    far = lax.ppermute(jnp.where(core == 0, low, high), "local", onward)
    return lax.ppermute(low, "local", swap), lax.ppermute(high, "local", swap), far


def hand_over(piece):
    members = lax.axis_size("local")
    return lax.ppermute(piece, "local", [(i, i ^ 1) for i in range(members)])


def piece_blocks(me, members):
    mate = me + 1 - 2 * (me % 2)
    blocks = [me, mate, me - 2, me + 2, mate - 2, mate + 2, me + 4, mate + 4]
    return jnp.stack([b % members for b in blocks])


def block_at(block):
    return pl.ds(pl.multiple_of(block * 128, 128), 128)


def back_kernel(partners_ref, *refs):
    pieces, hidden_ref, out_ref = refs[:8], refs[8], refs[9]
    left = jnp.concatenate([hidden_ref[block_at(partners_ref[k]), :] for k in range(8)], 1)

    @pl.loop(0, out_ref.shape[1] // TILE, unroll=True)
    def _(j):
        at = pl.ds(pl.multiple_of(j * TILE, TILE), TILE)
        right = jnp.concatenate([r[:, at] for r in pieces], 0)
        out_ref[:, at] = jnp.dot(left, right, preferred_element_type=jnp.float32)


IN_VMEM = pl.BlockSpec(memory_space=pltpu.VMEM)
IN_SMEM = pl.BlockSpec(memory_space=pltpu.SMEM)


def back_projection(partners, pieces, hidden_own):
    width = pieces[0].shape[1]
    return pl.pallas_call(
        back_kernel,
        in_specs=[IN_SMEM] + [IN_VMEM] * 9,
        out_specs=IN_VMEM,
        out_shape=jax.ShapeDtypeStruct((pieces[0].shape[0], width), jnp.float32),
        compiler_params=pltpu.CompilerParams(vmem_limit_bytes=VMEM_BYTES),
        cost_estimate=pl.CostEstimate(
            flops=2 * 128 * 1024 * width, bytes_accessed=10 * 128 * width * 2, transcendentals=0
        ),
        name="back_projection",
    )(partners, *pieces, hidden_own)


def own_slots(hidden_now, me):
    members = lax.axis_size("local")
    rows, units = hidden_now.shape
    held = hidden_now.reshape(2, 2, 2, rows // members, units)
    for axis, bit in ((2, 1), (1, 2), (0, 4)):
        mine = (me // bit) % 2
        low = lax.index_in_dim(held, 0, axis, keepdims=False)
        high = lax.index_in_dim(held, 1, axis, keepdims=False)
        keep = jnp.where(mine == 0, low, high)
        give = jnp.where(mine == 0, high, low)
        got = lax.ppermute(give, "local", [(i, i ^ bit) for i in range(members)])
        held = jnp.stack([keep, got], axis)
    return held.reshape(rows, units)


def piece_partners(me):
    even = 1 - (me // 2) % 2
    below = 2 + 4 * even
    above = 6 - 4 * even
    return jnp.stack([0 * me, 0 * me + 1, below, above, below + 1, above + 1, 0 * me + 4, 0 * me + 5])


def grad_kernel(count, start, final, blocks_ref, *refs):
    rows, refs = refs[:count], refs[count:]
    (hidden_t, weight_ref), refs = refs[:2], refs[2:]
    if final:
        part_ref, done_ref, second_ref, hidden_out, weight_out, second_out, total_u = refs
    else:
        part_out, total_out, total_u = refs
    left = jnp.concatenate([hidden_t[:, block_at(blocks_ref[start + k])] for k in range(count)], 1)
    total_u[...] = jnp.zeros_like(total_u)

    @pl.loop(0, weight_ref.shape[1] // TILE, unroll=True)
    def _(j):
        at = pl.ds(pl.multiple_of(j * TILE, TILE), TILE)
        weight_now = weight_ref[:, at]
        right = jnp.concatenate([r[:, at] for r in rows], 0)
        grad = jnp.dot(left, right, preferred_element_type=jnp.float32)
        total_u[...] += lax.dot_general(
            right, weight_now, (((1,), (1,)), ((), ())), preferred_element_type=jnp.float32
        )
        if not final:
            part_out[:, at] = grad
            return
        grad = grad + part_ref[:, at]
        second_new = beta_second * second_ref[:, at].astype(jnp.float32) + (1.0 - beta_second) * grad * grad
        weight_f = weight_now.astype(jnp.float32)
        update = grad / (jnp.sqrt(second_new * (1.0 / correct_second)) + epsilon) + decay_rate * weight_f
        weight_out[:, at] = (weight_f - learn_rate * update).astype(jnp.bfloat16)
        second_out[:, at] = second_new.astype(jnp.bfloat16)

    if not final:
        total_out[...] = total_u[...].astype(jnp.bfloat16)
        return
    for k in range(start + count):
        at = block_at(blocks_ref[k])
        if k < start:
            hidden_out[at, :] = done_ref[k * 128 : k * 128 + 128, :]
        else:
            hidden_out[at, :] = total_u[(k - start) * 128 : (k - start) * 128 + 128, :].astype(jnp.bfloat16)


def grads(blocks, pieces, start, hidden_t, weight_now, before=None, second_now=None):
    width = weight_now.shape[1]
    units, slots = hidden_t.shape
    count = len(pieces)
    final = before is not None
    if final:
        out_shape = [
            jax.ShapeDtypeStruct((slots, units), jnp.bfloat16),
            jax.ShapeDtypeStruct((units, width), jnp.bfloat16),
            jax.ShapeDtypeStruct((units, width), jnp.bfloat16),
        ]
        extra = (*before, second_now)
    else:
        out_shape = [
            jax.ShapeDtypeStruct((units, width), jnp.float32),
            jax.ShapeDtypeStruct((count * 128, units), jnp.bfloat16),
        ]
        extra = ()
    operands = (*pieces, hidden_t, weight_now, *extra)
    return pl.pallas_call(
        functools.partial(grad_kernel, count, start, final),
        in_specs=[IN_SMEM] + [IN_VMEM] * len(operands),
        out_specs=[IN_VMEM] * len(out_shape),
        out_shape=out_shape,
        scratch_shapes=[pltpu.VMEM((count * 128, units), jnp.float32)],
        compiler_params=pltpu.CompilerParams(vmem_limit_bytes=VMEM_BYTES),
        cost_estimate=pl.CostEstimate(
            flops=4 * 128 * 128 * count * width, bytes_accessed=(count + 6) * 128 * width * 2, transcendentals=0
        ),
        name="grads_last" if final else "grads_first",
    )(blocks, *operands)


def on_device(grad_out, expert_ids, gate_weights, saved_hidden, down_weight, second_moment):
    node_count = lax.axis_size("node")
    members = lax.axis_size("local")
    feature_count = grad_out.shape[1]
    me = lax.axis_index("local").astype(jnp.int32)
    expert_location, transit_rows, row_present, gate = route(expert_ids, gate_weights, node_count)
    slot_gate = jnp.sum(jnp.where(expert_location, gate[None, :], 0.0), 1)
    picked = jnp.dot(expert_location.astype(jnp.bfloat16), grad_out, preferred_element_type=jnp.float32)
    scaled_out = (slot_gate[:, None] * picked).astype(jnp.bfloat16)
    blocks = piece_blocks(me, members)
    leaving = scaled_out.reshape(node_count, CAP, feature_count)
    scaled = lax.all_to_all(leaving, "node", split_axis=0, concat_axis=0, tiled=True).reshape(
        node_count * CAP, feature_count
    )
    core = me % 2
    weight_now = down_weight[0]
    hidden_now = saved_hidden[0]
    hidden_t = hidden_now.T
    near = gather_near(weight_now)
    low, high, hidden_later = lax.optimization_barrier((near[2], near[3], hidden_now))
    more = gather_more(low, high, core)
    hidden_own = own_slots(hidden_later, me)
    far, hidden_own = lax.optimization_barrier((more[2], hidden_own))
    y = back_projection(piece_partners(me), near + more[:2] + (far, hand_over(far)), hidden_own)
    own_score = jnp.sum(scaled.astype(jnp.float32) * y, 1)
    returned = lax.all_to_all(
        own_score.reshape(node_count, CAP), "node", split_axis=0, concat_axis=0, tiled=True
    )
    near = gather_near(scaled)
    low, high, returned = lax.optimization_barrier((near[2], near[3], returned))
    more = gather_more(low, high, core)
    early = len(near)
    returned_flat = returned.reshape(node_count * CAP)
    token_score = jnp.sum(jnp.where(expert_location, returned_flat[:, None], 0.0), 0)
    token_gradient = jnp.where(row_present, token_score / jnp.where(row_present, gate, 1.0), 0.0)
    gate_weight_gradient = jnp.where(transit_rows, token_gradient[:, None], 0.0)
    other, gate_weight_gradient = lax.optimization_barrier((near[1], gate_weight_gradient))
    before = grads(blocks, (near[0], other, near[2], near[3]), 0, hidden_t, weight_now)
    far, before = lax.optimization_barrier((more[2], before))
    hidden_out, weight_new, second_new = grads(
        blocks, (more[0], more[1], far, hand_over(far)), early, hidden_t, weight_now, before, second_moment[0]
    )
    return (gate_weight_gradient, hidden_out[None], weight_new[None], second_new[None])


def solution(mesh):
    return jax.shard_map(
        on_device,
        mesh=mesh,
        in_specs=(
            P(("node", "local"), None),
            P(("node", "local"), None),
            P(("node", "local"), None),
            P("node", None, "local"),
            P("node", "local", None),
            P("node", "local", None),
        ),
        out_specs=(
            P(("node", "local"), None),
            P("node", None, "local"),
            P("node", "local", None),
            P("node", "local", None),
        ),
        check_vma=False,
    )
```

```python
import functools
import jax
import jax.numpy as jnp
from jax import lax
from jax.experimental import pallas as pl
from jax.experimental.pallas import tpu as pltpu
from jax.sharding import PartitionSpec as P

EXPERTS_PER_HOST = 4
CAP = 2
TILE = 896
VMEM_BYTES = 12 << 20


beta_second = 0.95
learn_rate = 0.002
decay_rate = 0.1
epsilon = 1e-08
correct_second = 0.994079470779666


def route(picked_experts, gate_values, node_count):
    transit_rows = picked_experts % EXPERTS_PER_HOST == 0
    row_present = jnp.any(transit_rows, 1)
    destination_node = jnp.sum(jnp.where(transit_rows, picked_experts // EXPERTS_PER_HOST, 0), 1)
    tokens = picked_experts.shape[0]
    same = (
        (destination_node[:, None] == destination_node[None, :])
        & row_present[None, :]
        & (jnp.arange(tokens)[None, :] < jnp.arange(tokens)[:, None])
    )
    within_rank = jnp.sum(same.astype(jnp.int32), 1)
    slot_index = destination_node * CAP + within_rank
    expert_location = (
        jnp.arange(node_count * CAP, dtype=jnp.int32)[:, None] == slot_index[None, :]
    ) & row_present[None, :]
    matched_gate = jnp.sum(jnp.where(transit_rows, gate_values, 0.0), 1).astype(jnp.bfloat16)
    return expert_location, transit_rows, row_present, matched_gate.astype(jnp.float32)


def gather_near(block):
    members = lax.axis_size("local")
    up = [(i, (i + 2) % members) for i in range(members)]
    down = [(i, (i - 2) % members) for i in range(members)]
    swap = [(i, i ^ 1) for i in range(members)]
    low = lax.ppermute(block, "local", up)
    high = lax.ppermute(block, "local", down)
    other = lax.ppermute(block, "local", swap)
    return block, other, low, high


def gather_more(low, high, core):
    members = lax.axis_size("local")
    onward = [(i, (i + (2 if i % 2 == 0 else -2)) % members) for i in range(members)]
    swap = [(i, i ^ 1) for i in range(members)]
    far = lax.ppermute(jnp.where(core == 0, low, high), "local", onward)
    return lax.ppermute(low, "local", swap), lax.ppermute(high, "local", swap), far


def hand_over(piece):
    members = lax.axis_size("local")
    return lax.ppermute(piece, "local", [(i, i ^ 1) for i in range(members)])


def piece_blocks(me, members):
    mate = me + 1 - 2 * (me % 2)
    blocks = [me, mate, me - 2, me + 2, mate - 2, mate + 2, me + 4, mate + 4]
    return jnp.stack([b % members for b in blocks])


def block_at(block):
    return pl.ds(pl.multiple_of(block * 128, 128), 128)


def back_kernel(partners_ref, *refs):
    pieces, hidden_ref, out_ref = refs[:8], refs[8], refs[9]
    left = jnp.concatenate([hidden_ref[block_at(partners_ref[k]), :] for k in range(8)], 1)

    @pl.loop(0, out_ref.shape[1] // TILE, unroll=True)
    def _(j):
        at = pl.ds(pl.multiple_of(j * TILE, TILE), TILE)
        right = jnp.concatenate([r[:, at] for r in pieces], 0)
        out_ref[:, at] = jnp.dot(left, right, preferred_element_type=jnp.float32)


IN_VMEM = pl.BlockSpec(memory_space=pltpu.VMEM)
IN_SMEM = pl.BlockSpec(memory_space=pltpu.SMEM)


def back_projection(partners, pieces, hidden_own):
    width = pieces[0].shape[1]
    return pl.pallas_call(
        back_kernel,
        in_specs=[IN_SMEM] + [IN_VMEM] * 9,
        out_specs=IN_VMEM,
        out_shape=jax.ShapeDtypeStruct((pieces[0].shape[0], width), jnp.float32),
        compiler_params=pltpu.CompilerParams(vmem_limit_bytes=VMEM_BYTES),
        cost_estimate=pl.CostEstimate(
            flops=2 * 128 * 1024 * width, bytes_accessed=10 * 128 * width * 2, transcendentals=0
        ),
        name="back_projection",
    )(partners, *pieces, hidden_own)


def own_slots(hidden_now, me):
    members = lax.axis_size("local")
    rows, units = hidden_now.shape
    held = hidden_now.reshape(2, 2, 2, rows // members, units)
    for axis, bit in ((2, 1), (1, 2), (0, 4)):
        mine = (me // bit) % 2
        low = lax.index_in_dim(held, 0, axis, keepdims=False)
        high = lax.index_in_dim(held, 1, axis, keepdims=False)
        keep = jnp.where(mine == 0, low, high)
        give = jnp.where(mine == 0, high, low)
        got = lax.ppermute(give, "local", [(i, i ^ bit) for i in range(members)])
        held = jnp.stack([keep, got], axis)
    return held.reshape(rows, units)


def piece_partners(me):
    even = 1 - (me // 2) % 2
    below = 2 + 4 * even
    above = 6 - 4 * even
    return jnp.stack([0 * me, 0 * me + 1, below, above, below + 1, above + 1, 0 * me + 4, 0 * me + 5])


def grad_kernel(count, start, final, blocks_ref, *refs):
    rows, refs = refs[:count], refs[count:]
    (hidden_t, weight_ref), refs = refs[:2], refs[2:]
    if final:
        part_ref, done_ref, second_ref, hidden_out, weight_out, second_out, total_u = refs
    else:
        part_out, total_out, total_u = refs
    left = jnp.concatenate([hidden_t[:, block_at(blocks_ref[start + k])] for k in range(count)], 1)
    total_u[...] = jnp.zeros_like(total_u)

    @pl.loop(0, weight_ref.shape[1] // TILE, unroll=True)
    def _(j):
        at = pl.ds(pl.multiple_of(j * TILE, TILE), TILE)
        weight_now = weight_ref[:, at]
        right = jnp.concatenate([r[:, at] for r in rows], 0)
        grad = jnp.dot(left, right, preferred_element_type=jnp.float32)
        total_u[...] += lax.dot_general(
            right, weight_now, (((1,), (1,)), ((), ())), preferred_element_type=jnp.float32
        )
        if not final:
            part_out[:, at] = grad
            return
        grad = grad + part_ref[:, at]
        second_new = beta_second * second_ref[:, at].astype(jnp.float32) + (1.0 - beta_second) * grad * grad
        weight_f = weight_now.astype(jnp.float32)
        update = grad / (jnp.sqrt(second_new * (1.0 / correct_second)) + epsilon) + decay_rate * weight_f
        weight_out[:, at] = (weight_f - learn_rate * update).astype(jnp.bfloat16)
        second_out[:, at] = second_new.astype(jnp.bfloat16)

    if not final:
        total_out[...] = total_u[...].astype(jnp.bfloat16)
        return
    for k in range(start + count):
        at = block_at(blocks_ref[k])
        if k < start:
            hidden_out[at, :] = done_ref[k * 128 : k * 128 + 128, :]
        else:
            hidden_out[at, :] = total_u[(k - start) * 128 : (k - start) * 128 + 128, :].astype(jnp.bfloat16)


def grads(blocks, pieces, start, hidden_t, weight_now, before=None, second_now=None):
    width = weight_now.shape[1]
    units, slots = hidden_t.shape
    count = len(pieces)
    final = before is not None
    if final:
        out_shape = [
            jax.ShapeDtypeStruct((slots, units), jnp.bfloat16),
            jax.ShapeDtypeStruct((units, width), jnp.bfloat16),
            jax.ShapeDtypeStruct((units, width), jnp.bfloat16),
        ]
        extra = (*before, second_now)
    else:
        out_shape = [
            jax.ShapeDtypeStruct((units, width), jnp.float32),
            jax.ShapeDtypeStruct((count * 128, units), jnp.bfloat16),
        ]
        extra = ()
    operands = (*pieces, hidden_t, weight_now, *extra)
    return pl.pallas_call(
        functools.partial(grad_kernel, count, start, final),
        in_specs=[IN_SMEM] + [IN_VMEM] * len(operands),
        out_specs=[IN_VMEM] * len(out_shape),
        out_shape=out_shape,
        scratch_shapes=[pltpu.VMEM((count * 128, units), jnp.float32)],
        compiler_params=pltpu.CompilerParams(vmem_limit_bytes=VMEM_BYTES),
        cost_estimate=pl.CostEstimate(
            flops=4 * 128 * 128 * count * width, bytes_accessed=(count + 6) * 128 * width * 2, transcendentals=0
        ),
        name="grads_last" if final else "grads_first",
    )(blocks, *operands)


def on_device(grad_out, expert_ids, gate_weights, saved_hidden, down_weight, second_moment):
    node_count = lax.axis_size("node")
    members = lax.axis_size("local")
    feature_count = grad_out.shape[1]
    me = lax.axis_index("local").astype(jnp.int32)
    expert_location, transit_rows, row_present, gate = route(expert_ids, gate_weights, node_count)
    slot_gate = jnp.sum(jnp.where(expert_location, gate[None, :], 0.0), 1)
    picked = jnp.dot(expert_location.astype(jnp.bfloat16), grad_out, preferred_element_type=jnp.float32)
    scaled_out = (slot_gate[:, None] * picked).astype(jnp.bfloat16)
    blocks = piece_blocks(me, members)
    leaving = scaled_out.reshape(node_count, CAP, feature_count)
    scaled = lax.all_to_all(leaving, "node", split_axis=0, concat_axis=0, tiled=True).reshape(
        node_count * CAP, feature_count
    )
    core = me % 2
    weight_now = down_weight[0]
    hidden_now = saved_hidden[0]
    hidden_t = hidden_now.T
    near = gather_near(weight_now)
    low, high, hidden_later = lax.optimization_barrier((near[2], near[3], hidden_now))
    more = gather_more(low, high, core)
    hidden_own = own_slots(hidden_later, me)
    far, hidden_own = lax.optimization_barrier((more[2], hidden_own))
    y = back_projection(piece_partners(me), near + more[:2] + (far, hand_over(far)), hidden_own)
    scaled, y = lax.optimization_barrier((scaled, y))
    own_score = jnp.sum(scaled.astype(jnp.float32) * y, 1)
    returned = lax.all_to_all(
        own_score.reshape(node_count, CAP), "node", split_axis=0, concat_axis=0, tiled=True
    )
    near = gather_near(scaled)
    low, high, returned = lax.optimization_barrier((near[2], near[3], returned))
    more = gather_more(low, high, core)
    early = len(near)
    returned_flat = returned.reshape(node_count * CAP)
    token_score = jnp.sum(jnp.where(expert_location, returned_flat[:, None], 0.0), 0)
    token_gradient = jnp.where(row_present, token_score / jnp.where(row_present, gate, 1.0), 0.0)
    gate_weight_gradient = jnp.where(transit_rows, token_gradient[:, None], 0.0)
    other, gate_weight_gradient = lax.optimization_barrier((near[1], gate_weight_gradient))
    before = grads(blocks, (near[0], other, near[2], near[3]), 0, hidden_t, weight_now)
    far, before = lax.optimization_barrier((more[2], before))
    hidden_out, weight_new, second_new = grads(
        blocks, (more[0], more[1], far, hand_over(far)), early, hidden_t, weight_now, before, second_moment[0]
    )
    return (gate_weight_gradient, hidden_out[None], weight_new[None], second_new[None])


def solution(mesh):
    return jax.shard_map(
        on_device,
        mesh=mesh,
        in_specs=(
            P(("node", "local"), None),
            P(("node", "local"), None),
            P(("node", "local"), None),
            P("node", None, "local"),
            P("node", "local", None),
            P("node", "local", None),
        ),
        out_specs=(
            P(("node", "local"), None),
            P("node", None, "local"),
            P("node", "local", None),
            P("node", "local", None),
        ),
        check_vma=False,
    )
```

```python
import functools
import jax
import jax.numpy as jnp
from jax import lax
from jax.experimental import pallas as pl
from jax.experimental.pallas import tpu as pltpu
from jax.sharding import PartitionSpec as P

EXPERTS_PER_HOST = 4
CAP = 2
TILE = 896
VMEM_BYTES = 12 << 20


beta_second = 0.95
learn_rate = 0.002
decay_rate = 0.1
epsilon = 1e-08
correct_second = 0.994079470779666


def route(picked_experts, gate_values, node_count):
    transit_rows = picked_experts % EXPERTS_PER_HOST == 0
    row_present = jnp.any(transit_rows, 1)
    destination_node = jnp.sum(jnp.where(transit_rows, picked_experts // EXPERTS_PER_HOST, 0), 1)
    tokens = picked_experts.shape[0]
    same = (
        (destination_node[:, None] == destination_node[None, :])
        & row_present[None, :]
        & (jnp.arange(tokens)[None, :] < jnp.arange(tokens)[:, None])
    )
    within_rank = jnp.sum(same.astype(jnp.int32), 1)
    slot_index = destination_node * CAP + within_rank
    expert_location = (
        jnp.arange(node_count * CAP, dtype=jnp.int32)[:, None] == slot_index[None, :]
    ) & row_present[None, :]
    matched_gate = jnp.sum(jnp.where(transit_rows, gate_values, 0.0), 1).astype(jnp.bfloat16)
    return expert_location, transit_rows, row_present, matched_gate.astype(jnp.float32)


def gather_ways(block):
    members = lax.axis_size("local")
    up = [(i, (i + 2) % members) for i in range(members)]
    down = [(i, (i - 2) % members) for i in range(members)]
    return lax.ppermute(block, "local", up), lax.ppermute(block, "local", down)


def go_on(low, high, core):
    members = lax.axis_size("local")
    onward = [(i, (i + (2 if i % 2 == 0 else -2)) % members) for i in range(members)]
    return lax.ppermute(jnp.where(core == 0, low, high), "local", onward)


def hand_over(piece):
    members = lax.axis_size("local")
    return lax.ppermute(piece, "local", [(i, i ^ 1) for i in range(members)])


def piece_blocks(me, members):
    mate = me + 1 - 2 * (me % 2)
    blocks = [me, mate, me - 2, me + 2, mate - 2, mate + 2, me + 4, mate + 4]
    return jnp.stack([b % members for b in blocks])


def block_at(block):
    return pl.ds(pl.multiple_of(block * 128, 128), 128)


def back_kernel(partners_ref, *refs):
    pieces, (hidden_ref, out_ref) = refs[:-2], refs[-2:]
    left = jnp.concatenate([hidden_ref[block_at(partners_ref[k]), :] for k in range(8)], 1)

    @pl.loop(0, out_ref.shape[1] // TILE, unroll=True)
    def _(j):
        at = pl.ds(pl.multiple_of(j * TILE, TILE), TILE)
        right = jnp.concatenate([r[:, at] for r in pieces], 0)
        out_ref[:, at] = jnp.dot(left, right, preferred_element_type=jnp.float32)


IN_VMEM = pl.BlockSpec(memory_space=pltpu.VMEM)
IN_SMEM = pl.BlockSpec(memory_space=pltpu.SMEM)


def back_projection(partners, pieces, hidden_own):
    width = pieces[0].shape[1]
    return pl.pallas_call(
        back_kernel,
        in_specs=[IN_SMEM] + [IN_VMEM] * (len(pieces) + 1),
        out_specs=IN_VMEM,
        out_shape=jax.ShapeDtypeStruct((pieces[0].shape[0], width), jnp.float32),
        compiler_params=pltpu.CompilerParams(vmem_limit_bytes=VMEM_BYTES),
        cost_estimate=pl.CostEstimate(
            flops=2 * 128 * 1024 * width, bytes_accessed=10 * 128 * width * 2, transcendentals=0
        ),
        name="back_projection",
    )(partners, *pieces, hidden_own)


def own_slots(hidden_now, me):
    members = lax.axis_size("local")
    rows, units = hidden_now.shape
    held = hidden_now.reshape(2, 2, 2, rows // members, units)
    for axis, bit in ((2, 1), (1, 2), (0, 4)):
        mine = (me // bit) % 2
        low = lax.index_in_dim(held, 0, axis, keepdims=False)
        high = lax.index_in_dim(held, 1, axis, keepdims=False)
        keep = jnp.where(mine == 0, low, high)
        give = jnp.where(mine == 0, high, low)
        got = lax.ppermute(give, "local", [(i, i ^ bit) for i in range(members)])
        held = jnp.stack([keep, got], axis)
    return held.reshape(rows, units)


def piece_partners(me):
    even = 1 - (me // 2) % 2
    below = 2 + 4 * even
    above = 6 - 4 * even
    return jnp.stack([0 * me, below, above, 0 * me + 1, below + 1, above + 1, 0 * me + 4, 0 * me + 5])


def grad_kernel(count, start, final, blocks_ref, *refs):
    rows, refs = refs[:count], refs[count:]
    (hidden_t, weight_ref), refs = refs[:2], refs[2:]
    if final:
        part_ref, done_ref, second_ref, hidden_out, weight_out, second_out, total_u = refs
    else:
        part_out, total_out, total_u = refs
    left = jnp.concatenate([hidden_t[:, block_at(blocks_ref[start + k])] for k in range(count)], 1)
    total_u[...] = jnp.zeros_like(total_u)

    @pl.loop(0, weight_ref.shape[1] // TILE, unroll=True)
    def _(j):
        at = pl.ds(pl.multiple_of(j * TILE, TILE), TILE)
        weight_now = weight_ref[:, at]
        right = jnp.concatenate([r[:, at] for r in rows], 0)
        grad = jnp.dot(left, right, preferred_element_type=jnp.float32)
        total_u[...] += lax.dot_general(
            right, weight_now, (((1,), (1,)), ((), ())), preferred_element_type=jnp.float32
        )
        if not final:
            part_out[:, at] = grad
            return
        grad = grad + part_ref[:, at]
        second_new = beta_second * second_ref[:, at].astype(jnp.float32) + (1.0 - beta_second) * grad * grad
        weight_f = weight_now.astype(jnp.float32)
        update = grad / (jnp.sqrt(second_new * (1.0 / correct_second)) + epsilon) + decay_rate * weight_f
        weight_out[:, at] = (weight_f - learn_rate * update).astype(jnp.bfloat16)
        second_out[:, at] = second_new.astype(jnp.bfloat16)

    if not final:
        total_out[...] = total_u[...].astype(jnp.bfloat16)
        return
    for k in range(start + count):
        at = block_at(blocks_ref[k])
        if k < start:
            hidden_out[at, :] = done_ref[k * 128 : k * 128 + 128, :]
        else:
            hidden_out[at, :] = total_u[(k - start) * 128 : (k - start) * 128 + 128, :].astype(jnp.bfloat16)


def grads(blocks, pieces, start, hidden_t, weight_now, before=None, second_now=None):
    width = weight_now.shape[1]
    units, slots = hidden_t.shape
    count = len(pieces)
    final = before is not None
    if final:
        out_shape = [
            jax.ShapeDtypeStruct((slots, units), jnp.bfloat16),
            jax.ShapeDtypeStruct((units, width), jnp.bfloat16),
            jax.ShapeDtypeStruct((units, width), jnp.bfloat16),
        ]
        extra = (*before, second_now)
    else:
        out_shape = [
            jax.ShapeDtypeStruct((units, width), jnp.float32),
            jax.ShapeDtypeStruct((count * 128, units), jnp.bfloat16),
        ]
        extra = ()
    operands = (*pieces, hidden_t, weight_now, *extra)
    return pl.pallas_call(
        functools.partial(grad_kernel, count, start, final),
        in_specs=[IN_SMEM] + [IN_VMEM] * len(operands),
        out_specs=[IN_VMEM] * len(out_shape),
        out_shape=out_shape,
        scratch_shapes=[pltpu.VMEM((count * 128, units), jnp.float32)],
        compiler_params=pltpu.CompilerParams(vmem_limit_bytes=VMEM_BYTES),
        cost_estimate=pl.CostEstimate(
            flops=4 * 128 * 128 * count * width, bytes_accessed=(count + 6) * 128 * width * 2, transcendentals=0
        ),
        name="grads_last" if final else "grads_first",
    )(blocks, *operands)


def on_device(grad_out, expert_ids, gate_weights, saved_hidden, down_weight, second_moment):
    node_count = lax.axis_size("node")
    members = lax.axis_size("local")
    feature_count = grad_out.shape[1]
    me = lax.axis_index("local").astype(jnp.int32)
    expert_location, transit_rows, row_present, gate = route(expert_ids, gate_weights, node_count)
    slot_gate = jnp.sum(jnp.where(expert_location, gate[None, :], 0.0), 1)
    picked = jnp.dot(expert_location.astype(jnp.bfloat16), grad_out, preferred_element_type=jnp.float32)
    scaled_out = (slot_gate[:, None] * picked).astype(jnp.bfloat16)
    blocks = piece_blocks(me, members)
    leaving = scaled_out.reshape(node_count, CAP, feature_count)
    weight_now, leaving = lax.optimization_barrier((down_weight[0], leaving))
    scaled = lax.all_to_all(leaving, "node", split_axis=0, concat_axis=0, tiled=True).reshape(
        node_count * CAP, feature_count
    )
    core = me % 2
    hidden_now = saved_hidden[0]
    hidden_t = hidden_now.T
    low, high = gather_ways(weight_now)
    low, high, hidden_later = lax.optimization_barrier((low, high, hidden_now))
    far = go_on(low, high, core)
    mates = hand_over(jnp.concatenate([weight_now, low, high], 0))
    hidden_own = own_slots(hidden_later, me)
    far, hidden_own = lax.optimization_barrier((far, hidden_own))
    y = back_projection(piece_partners(me), (weight_now, low, high, mates, far, hand_over(far)), hidden_own)
    scaled, y = lax.optimization_barrier((scaled, y))
    own_score = jnp.sum(scaled.astype(jnp.float32) * y, 1)
    returned = lax.all_to_all(
        own_score.reshape(node_count, CAP), "node", split_axis=0, concat_axis=0, tiled=True
    )
    low, high = gather_ways(scaled)
    near = (scaled, hand_over(scaled), low, high)
    low, high, returned = lax.optimization_barrier((low, high, returned))
    more = (hand_over(low), hand_over(high), go_on(low, high, core))
    early = len(near)
    returned_flat = returned.reshape(node_count * CAP)
    token_score = jnp.sum(jnp.where(expert_location, returned_flat[:, None], 0.0), 0)
    token_gradient = jnp.where(row_present, token_score / jnp.where(row_present, gate, 1.0), 0.0)
    gate_weight_gradient = jnp.where(transit_rows, token_gradient[:, None], 0.0)
    other, gate_weight_gradient = lax.optimization_barrier((near[1], gate_weight_gradient))
    before = grads(blocks, (near[0], other, near[2], near[3]), 0, hidden_t, weight_now)
    far, before = lax.optimization_barrier((more[2], before))
    hidden_out, weight_new, second_new = grads(
        blocks, (more[0], more[1], far, hand_over(far)), early, hidden_t, weight_now, before, second_moment[0]
    )
    return (gate_weight_gradient, hidden_out[None], weight_new[None], second_new[None])


def solution(mesh):
    return jax.shard_map(
        on_device,
        mesh=mesh,
        in_specs=(
            P(("node", "local"), None),
            P(("node", "local"), None),
            P(("node", "local"), None),
            P("node", None, "local"),
            P("node", "local", None),
            P("node", "local", None),
        ),
        out_specs=(
            P(("node", "local"), None),
            P("node", None, "local"),
            P("node", "local", None),
            P("node", "local", None),
        ),
        check_vma=False,
    )
```

```python
import functools
import jax
import jax.numpy as jnp
from jax import lax
from jax.experimental import pallas as pl
from jax.experimental.pallas import tpu as pltpu
from jax.sharding import PartitionSpec as P

EXPERTS_PER_HOST = 4
CAP = 2
TILE = 896
VMEM_BYTES = 12 << 20


beta_second = 0.95
learn_rate = 0.002
decay_rate = 0.1
epsilon = 1e-08
correct_second = 0.994079470779666


def route(picked_experts, gate_values, node_count):
    transit_rows = picked_experts % EXPERTS_PER_HOST == 0
    row_present = jnp.any(transit_rows, 1)
    destination_node = jnp.sum(jnp.where(transit_rows, picked_experts // EXPERTS_PER_HOST, 0), 1)
    tokens = picked_experts.shape[0]
    same = (
        (destination_node[:, None] == destination_node[None, :])
        & row_present[None, :]
        & (jnp.arange(tokens)[None, :] < jnp.arange(tokens)[:, None])
    )
    within_rank = jnp.sum(same.astype(jnp.int32), 1)
    slot_index = destination_node * CAP + within_rank
    expert_location = (
        jnp.arange(node_count * CAP, dtype=jnp.int32)[:, None] == slot_index[None, :]
    ) & row_present[None, :]
    matched_gate = jnp.sum(jnp.where(transit_rows, gate_values, 0.0), 1).astype(jnp.bfloat16)
    return expert_location, transit_rows, row_present, matched_gate.astype(jnp.float32)


def gather_ways(block):
    members = lax.axis_size("local")
    up = [(i, (i + 2) % members) for i in range(members)]
    down = [(i, (i - 2) % members) for i in range(members)]
    return lax.ppermute(block, "local", up), lax.ppermute(block, "local", down)


def go_on(low, high, core):
    members = lax.axis_size("local")
    onward = [(i, (i + (2 if i % 2 == 0 else -2)) % members) for i in range(members)]
    return lax.ppermute(jnp.where(core == 0, low, high), "local", onward)


def hand_over(piece):
    members = lax.axis_size("local")
    return lax.ppermute(piece, "local", [(i, i ^ 1) for i in range(members)])


def piece_blocks(me, members):
    mate = me + 1 - 2 * (me % 2)
    blocks = [me, mate, me - 2, me + 2, mate - 2, mate + 2, me + 4, mate + 4]
    return jnp.stack([b % members for b in blocks])


def block_at(block):
    return pl.ds(pl.multiple_of(block * 128, 128), 128)


def back_kernel(partners_ref, *refs):
    pieces, (hidden_ref, out_ref) = refs[:-2], refs[-2:]
    left = jnp.concatenate([hidden_ref[block_at(partners_ref[k]), :] for k in range(8)], 1)

    @pl.loop(0, out_ref.shape[1] // TILE, unroll=True)
    def _(j):
        at = pl.ds(pl.multiple_of(j * TILE, TILE), TILE)
        right = jnp.concatenate([r[:, at] for r in pieces], 0)
        out_ref[:, at] = jnp.dot(left, right, preferred_element_type=jnp.float32)


IN_VMEM = pl.BlockSpec(memory_space=pltpu.VMEM)
IN_SMEM = pl.BlockSpec(memory_space=pltpu.SMEM)


def back_projection(partners, pieces, hidden_own):
    width = pieces[0].shape[1]
    return pl.pallas_call(
        back_kernel,
        in_specs=[IN_SMEM] + [IN_VMEM] * (len(pieces) + 1),
        out_specs=IN_VMEM,
        out_shape=jax.ShapeDtypeStruct((pieces[0].shape[0], width), jnp.float32),
        compiler_params=pltpu.CompilerParams(vmem_limit_bytes=VMEM_BYTES),
        cost_estimate=pl.CostEstimate(
            flops=2 * 128 * 1024 * width, bytes_accessed=10 * 128 * width * 2, transcendentals=0
        ),
        name="back_projection",
    )(partners, *pieces, hidden_own)


def own_slots(hidden_now, me, stack, far):
    members = lax.axis_size("local")
    rows, units = hidden_now.shape
    held = hidden_now.reshape(2, 2, 2, rows // members, units)
    for axis, bit in ((2, 1), (1, 2), (0, 4)):
        mine = (me // bit) % 2
        low = lax.index_in_dim(held, 0, axis, keepdims=False)
        high = lax.index_in_dim(held, 1, axis, keepdims=False)
        keep = jnp.where(mine == 0, low, high)
        give = jnp.where(mine == 0, high, low)
        got = lax.ppermute(give, "local", [(i, i ^ bit) for i in range(members)])
        if bit == 1:
            got, *stack = lax.optimization_barrier((got, *stack))
            mates = hand_over(jnp.concatenate(stack, 0))
        if bit == 2:
            got, far = lax.optimization_barrier((got, far))
            far_mate = hand_over(far)
        held = jnp.stack([keep, got], axis)
    return held.reshape(rows, units), mates, far, far_mate


def piece_partners(me):
    even = 1 - (me // 2) % 2
    below = 2 + 4 * even
    above = 6 - 4 * even
    return jnp.stack([0 * me, below, above, 0 * me + 1, below + 1, above + 1, 0 * me + 4, 0 * me + 5])


def grad_kernel(count, start, final, blocks_ref, *refs):
    rows, refs = refs[:count], refs[count:]
    (hidden_t, weight_ref), refs = refs[:2], refs[2:]
    if final:
        part_ref, done_ref, second_ref, hidden_out, weight_out, second_out, total_u = refs
    else:
        part_out, total_out, total_u = refs
    left = jnp.concatenate([hidden_t[:, block_at(blocks_ref[start + k])] for k in range(count)], 1)
    total_u[...] = jnp.zeros_like(total_u)

    @pl.loop(0, weight_ref.shape[1] // TILE, unroll=True)
    def _(j):
        at = pl.ds(pl.multiple_of(j * TILE, TILE), TILE)
        weight_now = weight_ref[:, at]
        right = jnp.concatenate([r[:, at] for r in rows], 0)
        grad = jnp.dot(left, right, preferred_element_type=jnp.float32)
        total_u[...] += lax.dot_general(
            right, weight_now, (((1,), (1,)), ((), ())), preferred_element_type=jnp.float32
        )
        if not final:
            part_out[:, at] = grad
            return
        grad = grad + part_ref[:, at]
        second_new = beta_second * second_ref[:, at].astype(jnp.float32) + (1.0 - beta_second) * grad * grad
        weight_f = weight_now.astype(jnp.float32)
        update = grad / (jnp.sqrt(second_new * (1.0 / correct_second)) + epsilon) + decay_rate * weight_f
        weight_out[:, at] = (weight_f - learn_rate * update).astype(jnp.bfloat16)
        second_out[:, at] = second_new.astype(jnp.bfloat16)

    if not final:
        total_out[...] = total_u[...].astype(jnp.bfloat16)
        return
    for k in range(start + count):
        at = block_at(blocks_ref[k])
        if k < start:
            hidden_out[at, :] = done_ref[k * 128 : k * 128 + 128, :]
        else:
            hidden_out[at, :] = total_u[(k - start) * 128 : (k - start) * 128 + 128, :].astype(jnp.bfloat16)


def grads(blocks, pieces, start, hidden_t, weight_now, before=None, second_now=None):
    width = weight_now.shape[1]
    units, slots = hidden_t.shape
    count = len(pieces)
    final = before is not None
    if final:
        out_shape = [
            jax.ShapeDtypeStruct((slots, units), jnp.bfloat16),
            jax.ShapeDtypeStruct((units, width), jnp.bfloat16),
            jax.ShapeDtypeStruct((units, width), jnp.bfloat16),
        ]
        extra = (*before, second_now)
    else:
        out_shape = [
            jax.ShapeDtypeStruct((units, width), jnp.float32),
            jax.ShapeDtypeStruct((count * 128, units), jnp.bfloat16),
        ]
        extra = ()
    operands = (*pieces, hidden_t, weight_now, *extra)
    return pl.pallas_call(
        functools.partial(grad_kernel, count, start, final),
        in_specs=[IN_SMEM] + [IN_VMEM] * len(operands),
        out_specs=[IN_VMEM] * len(out_shape),
        out_shape=out_shape,
        scratch_shapes=[pltpu.VMEM((count * 128, units), jnp.float32)],
        compiler_params=pltpu.CompilerParams(vmem_limit_bytes=VMEM_BYTES),
        cost_estimate=pl.CostEstimate(
            flops=4 * 128 * 128 * count * width, bytes_accessed=(count + 6) * 128 * width * 2, transcendentals=0
        ),
        name="grads_last" if final else "grads_first",
    )(blocks, *operands)


def on_device(grad_out, expert_ids, gate_weights, saved_hidden, down_weight, second_moment):
    node_count = lax.axis_size("node")
    members = lax.axis_size("local")
    feature_count = grad_out.shape[1]
    me = lax.axis_index("local").astype(jnp.int32)
    expert_location, transit_rows, row_present, gate = route(expert_ids, gate_weights, node_count)
    slot_gate = jnp.sum(jnp.where(expert_location, gate[None, :], 0.0), 1)
    picked = jnp.dot(expert_location.astype(jnp.bfloat16), grad_out, preferred_element_type=jnp.float32)
    scaled_out = (slot_gate[:, None] * picked).astype(jnp.bfloat16)
    blocks = piece_blocks(me, members)
    leaving = scaled_out.reshape(node_count, CAP, feature_count)
    weight_now, leaving = lax.optimization_barrier((down_weight[0], leaving))
    scaled = lax.all_to_all(leaving, "node", split_axis=0, concat_axis=0, tiled=True).reshape(
        node_count * CAP, feature_count
    )
    core = me % 2
    hidden_now = saved_hidden[0]
    hidden_t = hidden_now.T
    low, high = gather_ways(weight_now)
    low, high, hidden_later = lax.optimization_barrier((low, high, hidden_now))
    far = go_on(low, high, core)
    hidden_own, mates, far, far_mate = own_slots(hidden_later, me, (weight_now, low, high), far)
    y = back_projection(piece_partners(me), (weight_now, low, high, mates, far, far_mate), hidden_own)
    scaled, y = lax.optimization_barrier((scaled, y))
    own_score = jnp.sum(scaled.astype(jnp.float32) * y, 1)
    returned = lax.all_to_all(
        own_score.reshape(node_count, CAP), "node", split_axis=0, concat_axis=0, tiled=True
    )
    low, high = gather_ways(scaled)
    near = (scaled, hand_over(scaled), low, high)
    low, high, returned = lax.optimization_barrier((low, high, returned))
    more = (hand_over(low), hand_over(high), go_on(low, high, core))
    early = len(near)
    returned_flat = returned.reshape(node_count * CAP)
    token_score = jnp.sum(jnp.where(expert_location, returned_flat[:, None], 0.0), 0)
    token_gradient = jnp.where(row_present, token_score / jnp.where(row_present, gate, 1.0), 0.0)
    gate_weight_gradient = jnp.where(transit_rows, token_gradient[:, None], 0.0)
    other, gate_weight_gradient = lax.optimization_barrier((near[1], gate_weight_gradient))
    before = grads(blocks, (near[0], other, near[2], near[3]), 0, hidden_t, weight_now)
    far, before = lax.optimization_barrier((more[2], before))
    hidden_out, weight_new, second_new = grads(
        blocks, (more[0], more[1], far, hand_over(far)), early, hidden_t, weight_now, before, second_moment[0]
    )
    return (gate_weight_gradient, hidden_out[None], weight_new[None], second_new[None])


def solution(mesh):
    return jax.shard_map(
        on_device,
        mesh=mesh,
        in_specs=(
            P(("node", "local"), None),
            P(("node", "local"), None),
            P(("node", "local"), None),
            P("node", None, "local"),
            P("node", "local", None),
            P("node", "local", None),
        ),
        out_specs=(
            P(("node", "local"), None),
            P("node", None, "local"),
            P("node", "local", None),
            P("node", "local", None),
        ),
        check_vma=False,
    )
```

```python
import functools
import jax
import jax.numpy as jnp
from jax import lax
from jax.experimental import pallas as pl
from jax.experimental.pallas import tpu as pltpu
from jax.sharding import PartitionSpec as P

EXPERTS_PER_HOST = 4
CAP = 2
TILE = 896
VMEM_BYTES = 12 << 20


beta_second = 0.95
learn_rate = 0.002
decay_rate = 0.1
epsilon = 1e-08
correct_second = 0.994079470779666


def route(picked_experts, gate_values, node_count):
    transit_rows = picked_experts % EXPERTS_PER_HOST == 0
    row_present = jnp.any(transit_rows, 1)
    destination_node = jnp.sum(jnp.where(transit_rows, picked_experts // EXPERTS_PER_HOST, 0), 1)
    tokens = picked_experts.shape[0]
    same = (
        (destination_node[:, None] == destination_node[None, :])
        & row_present[None, :]
        & (jnp.arange(tokens)[None, :] < jnp.arange(tokens)[:, None])
    )
    within_rank = jnp.sum(same.astype(jnp.int32), 1)
    slot_index = destination_node * CAP + within_rank
    expert_location = (
        jnp.arange(node_count * CAP, dtype=jnp.int32)[:, None] == slot_index[None, :]
    ) & row_present[None, :]
    matched_gate = jnp.sum(jnp.where(transit_rows, gate_values, 0.0), 1).astype(jnp.bfloat16)
    return expert_location, transit_rows, row_present, matched_gate.astype(jnp.float32)


def gather_ways(block):
    members = lax.axis_size("local")
    up = [(i, (i + 2) % members) for i in range(members)]
    down = [(i, (i - 2) % members) for i in range(members)]
    return lax.ppermute(block, "local", up), lax.ppermute(block, "local", down)


def go_on(low, high, core):
    members = lax.axis_size("local")
    onward = [(i, (i + (2 if i % 2 == 0 else -2)) % members) for i in range(members)]
    return lax.ppermute(jnp.where(core == 0, low, high), "local", onward)


def hand_over(piece):
    members = lax.axis_size("local")
    return lax.ppermute(piece, "local", [(i, i ^ 1) for i in range(members)])


def piece_blocks(me, members):
    mate = me + 1 - 2 * (me % 2)
    blocks = [me, mate, me - 2, me + 2, mate - 2, mate + 2, me + 4, mate + 4]
    return jnp.stack([b % members for b in blocks])


def block_at(block):
    return pl.ds(pl.multiple_of(block * 128, 128), 128)


def back_kernel(partners_ref, *refs):
    pieces, (hidden_ref, out_ref) = refs[:-2], refs[-2:]
    left = jnp.concatenate([hidden_ref[block_at(partners_ref[k]), :] for k in range(8)], 1)

    @pl.loop(0, out_ref.shape[1] // TILE, unroll=True)
    def _(j):
        at = pl.ds(pl.multiple_of(j * TILE, TILE), TILE)
        right = jnp.concatenate([r[:, at] for r in pieces], 0)
        out_ref[:, at] = jnp.dot(left, right, preferred_element_type=jnp.float32)


IN_VMEM = pl.BlockSpec(memory_space=pltpu.VMEM)
IN_SMEM = pl.BlockSpec(memory_space=pltpu.SMEM)


def back_projection(partners, pieces, hidden_own):
    width = pieces[0].shape[1]
    return pl.pallas_call(
        back_kernel,
        in_specs=[IN_SMEM] + [IN_VMEM] * (len(pieces) + 1),
        out_specs=IN_VMEM,
        out_shape=jax.ShapeDtypeStruct((pieces[0].shape[0], width), jnp.float32),
        compiler_params=pltpu.CompilerParams(vmem_limit_bytes=VMEM_BYTES),
        cost_estimate=pl.CostEstimate(
            flops=2 * 128 * 1024 * width, bytes_accessed=10 * 128 * width * 2, transcendentals=0
        ),
        name="back_projection",
    )(partners, *pieces, hidden_own)


def own_slots(hidden_now, me):
    members = lax.axis_size("local")
    rows, units = hidden_now.shape
    held = hidden_now.reshape(2, 2, 2, rows // members, units)
    for axis, bit in ((2, 1), (1, 2), (0, 4)):
        mine = (me // bit) % 2
        low = lax.index_in_dim(held, 0, axis, keepdims=False)
        high = lax.index_in_dim(held, 1, axis, keepdims=False)
        keep = jnp.where(mine == 0, low, high)
        give = jnp.where(mine == 0, high, low)
        got = lax.ppermute(give, "local", [(i, i ^ bit) for i in range(members)])
        held = jnp.stack([keep, got], axis)
    return held.reshape(rows, units)


def piece_partners(me):
    even = 1 - (me // 2) % 2
    below = 2 + 4 * even
    above = 6 - 4 * even
    return jnp.stack([0 * me, below, above, 0 * me + 1, below + 1, above + 1, 0 * me + 4, 0 * me + 5])


def grad_kernel(count, start, final, blocks_ref, *refs):
    rows, refs = refs[:count], refs[count:]
    (hidden_t, weight_ref), refs = refs[:2], refs[2:]
    if final:
        part_ref, done_ref, second_ref, hidden_out, weight_out, second_out, total_u = refs
    else:
        part_out, total_out, total_u = refs
    left = jnp.concatenate([hidden_t[:, block_at(blocks_ref[start + k])] for k in range(count)], 1)
    total_u[...] = jnp.zeros_like(total_u)

    @pl.loop(0, weight_ref.shape[1] // TILE, unroll=True)
    def _(j):
        at = pl.ds(pl.multiple_of(j * TILE, TILE), TILE)
        weight_now = weight_ref[:, at]
        right = jnp.concatenate([r[:, at] for r in rows], 0)
        grad = jnp.dot(left, right, preferred_element_type=jnp.float32)
        total_u[...] += lax.dot_general(
            right, weight_now, (((1,), (1,)), ((), ())), preferred_element_type=jnp.float32
        )
        if not final:
            part_out[:, at] = grad
            return
        grad = grad + part_ref[:, at]
        second_new = beta_second * second_ref[:, at].astype(jnp.float32) + (1.0 - beta_second) * grad * grad
        weight_f = weight_now.astype(jnp.float32)
        corrected = second_new * (1.0 / correct_second)
        update = grad / (corrected * lax.rsqrt(corrected) + epsilon) + decay_rate * weight_f
        weight_out[:, at] = (weight_f - learn_rate * update).astype(jnp.bfloat16)
        second_out[:, at] = second_new.astype(jnp.bfloat16)

    if not final:
        total_out[...] = total_u[...].astype(jnp.bfloat16)
        return
    for k in range(start + count):
        at = block_at(blocks_ref[k])
        if k < start:
            hidden_out[at, :] = done_ref[k * 128 : k * 128 + 128, :]
        else:
            hidden_out[at, :] = total_u[(k - start) * 128 : (k - start) * 128 + 128, :].astype(jnp.bfloat16)


def grads(blocks, pieces, start, hidden_t, weight_now, before=None, second_now=None):
    width = weight_now.shape[1]
    units, slots = hidden_t.shape
    count = len(pieces)
    final = before is not None
    if final:
        out_shape = [
            jax.ShapeDtypeStruct((slots, units), jnp.bfloat16),
            jax.ShapeDtypeStruct((units, width), jnp.bfloat16),
            jax.ShapeDtypeStruct((units, width), jnp.bfloat16),
        ]
        extra = (*before, second_now)
    else:
        out_shape = [
            jax.ShapeDtypeStruct((units, width), jnp.float32),
            jax.ShapeDtypeStruct((count * 128, units), jnp.bfloat16),
        ]
        extra = ()
    operands = (*pieces, hidden_t, weight_now, *extra)
    return pl.pallas_call(
        functools.partial(grad_kernel, count, start, final),
        in_specs=[IN_SMEM] + [IN_VMEM] * len(operands),
        out_specs=[IN_VMEM] * len(out_shape),
        out_shape=out_shape,
        scratch_shapes=[pltpu.VMEM((count * 128, units), jnp.float32)],
        compiler_params=pltpu.CompilerParams(vmem_limit_bytes=VMEM_BYTES),
        cost_estimate=pl.CostEstimate(
            flops=4 * 128 * 128 * count * width, bytes_accessed=(count + 6) * 128 * width * 2, transcendentals=0
        ),
        name="grads_last" if final else "grads_first",
    )(blocks, *operands)


def on_device(grad_out, expert_ids, gate_weights, saved_hidden, down_weight, second_moment):
    node_count = lax.axis_size("node")
    members = lax.axis_size("local")
    feature_count = grad_out.shape[1]
    me = lax.axis_index("local").astype(jnp.int32)
    expert_location, transit_rows, row_present, gate = route(expert_ids, gate_weights, node_count)
    slot_gate = jnp.sum(jnp.where(expert_location, gate[None, :], 0.0), 1)
    picked = jnp.dot(expert_location.astype(jnp.bfloat16), grad_out, preferred_element_type=jnp.float32)
    scaled_out = (slot_gate[:, None] * picked).astype(jnp.bfloat16)
    blocks = piece_blocks(me, members)
    leaving = scaled_out.reshape(node_count, CAP, feature_count)
    weight_now, leaving = lax.optimization_barrier((down_weight[0], leaving))
    scaled = lax.all_to_all(leaving, "node", split_axis=0, concat_axis=0, tiled=True).reshape(
        node_count * CAP, feature_count
    )
    core = me % 2
    hidden_now = saved_hidden[0]
    hidden_t = hidden_now.T
    low, high = gather_ways(weight_now)
    low, high, hidden_later = lax.optimization_barrier((low, high, hidden_now))
    far = go_on(low, high, core)
    mates = hand_over(jnp.concatenate([weight_now, low, high], 0))
    hidden_own = own_slots(hidden_later, me)
    far, hidden_own = lax.optimization_barrier((far, hidden_own))
    y = back_projection(piece_partners(me), (weight_now, low, high, mates, far, hand_over(far)), hidden_own)
    scaled, y = lax.optimization_barrier((scaled, y))
    own_score = jnp.sum(scaled.astype(jnp.float32) * y, 1)
    returned = lax.all_to_all(
        own_score.reshape(node_count, CAP), "node", split_axis=0, concat_axis=0, tiled=True
    )
    low, high = gather_ways(scaled)
    near = (scaled, hand_over(scaled), low, high)
    low, high, returned = lax.optimization_barrier((low, high, returned))
    more = (hand_over(low), hand_over(high), go_on(low, high, core))
    early = len(near)
    returned_flat = returned.reshape(node_count * CAP)
    token_score = jnp.sum(jnp.where(expert_location, returned_flat[:, None], 0.0), 0)
    token_gradient = jnp.where(row_present, token_score / jnp.where(row_present, gate, 1.0), 0.0)
    gate_weight_gradient = jnp.where(transit_rows, token_gradient[:, None], 0.0)
    other, gate_weight_gradient = lax.optimization_barrier((near[1], gate_weight_gradient))
    before = grads(blocks, (near[0], other, near[2], near[3]), 0, hidden_t, weight_now)
    far, before = lax.optimization_barrier((more[2], before))
    hidden_out, weight_new, second_new = grads(
        blocks, (more[0], more[1], far, hand_over(far)), early, hidden_t, weight_now, before, second_moment[0]
    )
    return (gate_weight_gradient, hidden_out[None], weight_new[None], second_new[None])


def solution(mesh):
    return jax.shard_map(
        on_device,
        mesh=mesh,
        in_specs=(
            P(("node", "local"), None),
            P(("node", "local"), None),
            P(("node", "local"), None),
            P("node", None, "local"),
            P("node", "local", None),
            P("node", "local", None),
        ),
        out_specs=(
            P(("node", "local"), None),
            P("node", None, "local"),
            P("node", "local", None),
            P("node", "local", None),
        ),
        check_vma=False,
    )
```
